32 devices in a mesh: group: 2 (over x), col: 16 (over z, y, core).
Axes of the slice: x: 2, y: 2, z: 4, core: 2. Of those that a mesh axis runs over, the one named last changes fastest.
Arguments:
- homolog_embedding: bfloat16 [192, 64, 256], P('group', 'col'), parts along dimension 0, may hold values from -6 to 6
- left_factor_matrix: bfloat16 [256, 32], replicated, may hold values from -0.375 to 0.375
- right_factor_matrix: bfloat16 [256, 32], replicated, may hold values from -0.375 to 0.375
- decoder: bfloat16 [1024, 128], replicated, may hold values from -2 to 2
- pair_output_bias: float32 [128], replicated, may hold values from -3 to 3
- pair_output_gradient: bfloat16 [128, 64, 128], P('group', 'col'), parts along dimension 0, may hold values from -6 to 6
Outputs:
- first_operand_gradient: float32 [192, 64, 32], P('group', 'col'), parts along dimension 0
- second_operand_gradient: float32 [192, 64, 32], P('group', 'col'), parts along dimension 0
- alignment_gradient: bfloat16 [192, 64, 256], P('group', 'col'), parts along dimension 0
The draws below stay inside these ranges and needn't reach their ends.
There are 2 independent parts, one for each index of `group`. The reference program is written for one: setup_inputs(seed, part) draws one part's arguments, and reference() takes and returns one part's arrays. A program takes and returns all parts, laid end to end along the dimension named above; an argument that names none is the same for every part. Nothing has to cross between parts.
All inputs are finite; a program needn't handle non-finite values.
Results may differ from the reference program's by a relative error of at most 0.0083.
Values may be sent and summed in bfloat16 or wider, within the bound.
A program may use at most 64 MiB of HBM per device.

```python
import jax
import jax.numpy as jnp
from jax import lax

EMBED_DEPTH = 256
FACTOR_DEPTH = 32
C_Z = 128
HOMOLOG_TALLY = 96
LOCAL_RESIDUES = 4
POSITION_TALLY = 64


def raised(values, stream_key, source, target, blocks, factor):
    owner, partner = [(jnp.arange(values.shape[position]) // (values.shape[position] // blocks)).reshape([-1 if axis == position else 1 for axis in range(values.ndim)]) for position in (source, target)]
    chosen = jax.random.permutation(stream_key, blocks)[partner]
    strong = (owner == chosen) | (owner == (partner + blocks // 2) % blocks)
    return jnp.where(strong, factor * values, values)


def block_levels(own_key, extent, shards, smallest, largest):
    level = 1.0
    for dim, shards_of in shards:
        steps = jax.random.uniform(jax.random.fold_in(jax.random.fold_in(own_key, 6), dim), (shards_of,), jnp.float32, smallest / len(shards), largest / len(shards))
        level = level * jnp.repeat(jnp.exp(steps), extent[dim] // shards_of).reshape((-1,) + (1,) * (len(extent) - 1 - dim))
    return level


def normal_values(rng, dims, scale, reach, shards=(), dtype=jnp.bfloat16):
    values = scale * jax.random.normal(rng, dims, jnp.float32)
    if shards:
        values = values * block_levels(rng, dims, shards, -0.22, 0.18)
    return jnp.clip(values, -reach, reach).astype(dtype)


def gaussian_with(stream_key, extent, scale, reach, cuts, heavy, kind=jnp.bfloat16):
    entries = scale * jax.random.normal(stream_key, extent, jnp.float32)
    if cuts:
        entries = entries * block_levels(stream_key, extent, cuts, -0.22, 0.18)
    return jnp.clip(raised(entries, jax.random.fold_in(stream_key, 3), *heavy), -reach, reach).astype(kind)


def setup_inputs(seed: int = 0, part: int = 0) -> dict:
    key_list = jax.random.split(jax.random.key(seed), 7)
    part_splits = jax.random.split(jax.random.fold_in(key_list[6], part), 7)
    return {
        "homolog_embedding": normal_values(part_splits[0], (HOMOLOG_TALLY, POSITION_TALLY, EMBED_DEPTH), 1.0, 6.0, ((1, 16),)),
        "left_factor_matrix": normal_values(key_list[1], (EMBED_DEPTH, FACTOR_DEPTH), EMBED_DEPTH ** -0.5, 0.375),
        "right_factor_matrix": normal_values(key_list[2], (EMBED_DEPTH, FACTOR_DEPTH), EMBED_DEPTH ** -0.5, 0.375),
        "decoder": normal_values(key_list[3], (FACTOR_DEPTH * FACTOR_DEPTH, C_Z), (FACTOR_DEPTH * FACTOR_DEPTH // HOMOLOG_TALLY) ** -0.5, 2.0),
        "pair_output_bias": normal_values(key_list[4], (C_Z,), 0.5, 3.0, (), jnp.float32),
        "pair_output_gradient": gaussian_with(part_splits[5], (POSITION_TALLY, POSITION_TALLY, C_Z), 1.0, 6.0, ((1, 16),), (1, 0, 16, 2.0)),
    }


def reference(homolog_embedding, left_factor_matrix, right_factor_matrix, decoder, pair_output_bias, pair_output_gradient):
    alignment_row_count, residue_length, alignment_channel_width = homolog_embedding.shape
    operand_channel_width = left_factor_matrix.shape[1]
    channels = decoder.shape[1]
    reciprocal_rows = 1.0 / alignment_row_count
    alignment_flattened_rows = homolog_embedding.reshape(alignment_row_count * residue_length, alignment_channel_width)
    first_operand_rows = jnp.dot(alignment_flattened_rows, left_factor_matrix, preferred_element_type=jnp.float32).astype(jnp.bfloat16).reshape(alignment_row_count, residue_length, operand_channel_width)
    second_operand_rows = jnp.dot(alignment_flattened_rows, right_factor_matrix, preferred_element_type=jnp.float32).astype(jnp.bfloat16).reshape(alignment_row_count, residue_length, operand_channel_width)
    count_of_blocks = residue_length // LOCAL_RESIDUES
    first_operand_blocks = first_operand_rows.reshape(alignment_row_count, count_of_blocks, LOCAL_RESIDUES, operand_channel_width).transpose(1, 0, 2, 3)
    cot_blocks = pair_output_gradient.reshape(count_of_blocks, LOCAL_RESIDUES, residue_length, channels)
    right_wide = second_operand_rows.astype(jnp.float32)

    def one_block(state_sum, items):
        left_block, upstream = items
        products = jnp.einsum("sic,sjd->ijcd", left_block.astype(jnp.float32), right_wide) * reciprocal_rows
        products = products.astype(jnp.bfloat16).reshape(LOCAL_RESIDUES * residue_length, operand_channel_width * operand_channel_width)
        linear = jnp.dot(products, decoder, preferred_element_type=jnp.float32) + pair_output_bias
        pre_slopes = (upstream.reshape(LOCAL_RESIDUES * residue_length, channels).astype(jnp.float32) * 2.0 * jnp.maximum(linear, 0.0)).astype(jnp.bfloat16)
        backward = jnp.dot(pre_slopes, decoder.T, preferred_element_type=jnp.float32) * reciprocal_rows
        slopes = backward.astype(jnp.bfloat16).reshape(LOCAL_RESIDUES, residue_length, operand_channel_width, operand_channel_width).astype(jnp.float32)
        left_grad = jnp.einsum("ijcd,sjd->sic", slopes, right_wide)
        state_sum = state_sum + jnp.einsum("ijcd,sic->sjd", slopes, left_block.astype(jnp.float32))
        return state_sum, left_grad

    starting_carry = jnp.zeros((alignment_row_count, residue_length, operand_channel_width), jnp.float32)
    second_operand_gradient, first_operand_pieces = lax.scan(one_block, starting_carry, (first_operand_blocks, cot_blocks))
    first_operand_gradient = first_operand_pieces.transpose(1, 0, 2, 3).reshape(alignment_row_count, residue_length, operand_channel_width)
    first_operand_gradient_step = first_operand_gradient.astype(jnp.bfloat16).reshape(alignment_row_count * residue_length, operand_channel_width)
    second_operand_gradient_step = second_operand_gradient.astype(jnp.bfloat16).reshape(alignment_row_count * residue_length, operand_channel_width)
    alignment_gradient = jnp.dot(first_operand_gradient_step, left_factor_matrix.T, preferred_element_type=jnp.float32) + jnp.dot(second_operand_gradient_step, right_factor_matrix.T, preferred_element_type=jnp.float32)
    alignment_gradient = alignment_gradient.astype(jnp.bfloat16).reshape(alignment_row_count, residue_length, alignment_channel_width)
    return first_operand_gradient, second_operand_gradient, alignment_gradient
```

```python
import functools

import jax
import jax.numpy as jnp
from jax import lax
from jax.experimental import pallas as pl
from jax.experimental.pallas import tpu as pltpu
from jax.sharding import PartitionSpec as P

MESH = pl.DeviceIdType.MESH
F32 = jnp.float32
BF16 = jnp.bfloat16


def dot(x, y, dims=((1,), (0,))):
    return lax.dot_general(x, y, (dims, ((), ())), preferred_element_type=F32)


NT = ((1,), (1,))
TN = ((0,), (0,))


def kernel(
    inner,
    outer,
    e_ref,
    wl_ref,
    wr_ref,
    dec_ref,
    bias_ref,
    g_ref,
    first_ref,
    second_ref,
    align_ref,
    lbuf,
    rbuf,
    gbuf,
    fown,
    sown,
    fsend,
    ssend,
    fbuf,
    sbuf,
    wpad,
    bd,
    perm,
    gf,
    mt,
    s2,
    l_ss,
    l_rs,
    r_ss,
    r_rs,
    g_ss,
    g_rs,
    f_ss,
    f_rs,
    s_ss,
    s_rs,
    own_sem,
):
    rows, res, width = e_ref.shape
    fac = wl_ref.shape[0]
    chan = dec_ref.shape[1]
    blk = res * fac
    ni = outer * res
    recip = 1.0 / rows
    me = lax.axis_index("col")
    a = lax.rem(me, inner)
    b = me // inner

    inner_peers = [lax.rem(a + k, inner) for k in range(1, inner)]
    outer_peers = [lax.rem(b + k, outer) for k in range(1, outer)]

    def inner_dev(p):
        return {"col": b * inner + p}

    def outer_dev(p):
        return {"col": p * inner + a}

    barrier = pltpu.get_barrier_semaphore()
    for p in outer_peers:
        pl.semaphore_signal(barrier, inc=1, device_id=outer_dev(p), device_id_type=MESH)
    for p in inner_peers:
        pl.semaphore_signal(barrier, inc=1, device_id=inner_dev(p), device_id_type=MESH)

    own_g = pltpu.make_async_copy(g_ref.at[:, pl.ds(a * res, res)], gbuf.at[a], own_sem)
    own_g.start()

    wpad[...] = jnp.zeros_like(wpad)
    for r in range(res):
        wpad[r, r * fac : (r + 1) * fac, :] = wl_ref[...]
        wpad[r, blk + r * fac : blk + (r + 1) * fac, :] = wr_ref[...]
    acc = dot(e_ref[:, 0, :], wpad[0], NT)
    for r in range(1, res):
        acc = acc + dot(e_ref[:, r, :], wpad[r], NT)
    acc = acc.astype(BF16)
    lbuf[b] = acc[:, :blk]
    rbuf[a] = acc[:, blk:]

    pl.semaphore_wait(barrier, inner + outer - 2)

    def send(src, dst, ss, rs, dev):
        c = pltpu.make_async_remote_copy(
            src_ref=src, dst_ref=dst, send_sem=ss, recv_sem=rs, device_id=dev, device_id_type=MESH
        )
        c.start()
        return c

    sends = []
    for k, p in enumerate(outer_peers):
        sends.append(send(lbuf.at[b], lbuf.at[b], l_ss.at[k], l_rs.at[b], outer_dev(p)))
    for k, p in enumerate(inner_peers):
        sends.append(send(rbuf.at[a], rbuf.at[a], r_ss.at[k], r_rs.at[a], inner_dev(p)))
    for k, p in enumerate(inner_peers):
        sends.append(
            send(
                g_ref.at[:, pl.ds(p * res, res)], gbuf.at[a], g_ss.at[k], g_rs.at[a], inner_dev(p)
            )
        )

    def arrive(buf, rs, p, dev):
        pltpu.make_async_remote_copy(
            src_ref=buf.at[p],
            dst_ref=buf.at[p],
            send_sem=rs.at[p],
            recv_sem=rs.at[p],
            device_id=dev,
            device_id_type=MESH,
        ).wait_recv()

    bd[...] = jnp.zeros_like(bd)
    for c in range(fac):
        piece = dec_ref[c * fac : (c + 1) * fac, :]
        for r in range(res):
            bd[c * blk + r * fac : c * blk + (r + 1) * fac, r * chan : (r + 1) * chan] = piece
    out_pos = lax.broadcasted_iota(jnp.int32, perm.shape, 0)
    in_pos = lax.broadcasted_iota(jnp.int32, perm.shape, 1)
    hit = in_pos == lax.rem(out_pos, ni) * fac + out_pos // ni
    perm[...] = jnp.where(hit, 1.0, 0.0).astype(BF16)

    own_g.wait()
    for p in outer_peers:
        arrive(lbuf, l_rs, p, outer_dev(p))
    left = jnp.concatenate([lbuf[q] for q in range(outer)], axis=1)
    left_p = dot(left, perm[...], NT).astype(BF16)

    for p in inner_peers:
        arrive(rbuf, r_rs, p, inner_dev(p))
    right = jnp.concatenate([rbuf[q] for q in range(inner)], axis=1)
    prod = (dot(left_p, right, TN) * recip).astype(BF16)
    for c in range(fac):
        for q in range(inner):
            mt[q * ni : (q + 1) * ni, c * blk : (c + 1) * blk] = prod[
                c * ni : (c + 1) * ni, q * blk : (q + 1) * blk
            ]
    for p in inner_peers:
        arrive(gbuf, g_rs, p, inner_dev(p))
    for q in range(inner):
        up = gbuf[q].reshape(ni, res, chan).astype(F32)
        for r in range(res):
            gf[q * ni : (q + 1) * ni, r * chan : (r + 1) * chan] = up[:, r, :]
    bias = jnp.concatenate([bias_ref[...]] * res, axis=1)
    linear = dot(mt[...], bd[...]) + bias
    pre = (gf[...] * 2.0 * jnp.maximum(linear, 0.0)).astype(BF16)
    slopes = (dot(pre, bd[...], NT) * recip).astype(BF16)
    for c in range(fac):
        for q in range(inner):
            s2[c * ni : (c + 1) * ni, q * blk : (q + 1) * blk] = slopes[
                q * ni : (q + 1) * ni, c * blk : (c + 1) * blk
            ]

    first_part = dot(right, s2[...], NT).astype(BF16)
    first_part = dot(first_part, perm[...])
    for q in range(outer):
        term = first_part[:, q * blk : (q + 1) * blk]
        fown[q] = term
        fsend[q] = term.astype(BF16)
    for k, p in enumerate(outer_peers):
        sends.append(send(fsend.at[p], fbuf.at[b], f_ss.at[k], f_rs.at[b], outer_dev(p)))
    second_part = dot(left_p, s2[...])
    for q in range(inner):
        term = second_part[:, q * blk : (q + 1) * blk]
        sown[q] = term
        ssend[q] = term.astype(BF16)
    for k, p in enumerate(inner_peers):
        sends.append(send(ssend.at[p], sbuf.at[a], s_ss.at[k], s_rs.at[a], inner_dev(p)))

    second = sown[a]
    for p in inner_peers:
        arrive(sbuf, s_rs, p, inner_dev(p))
        second = second + sbuf[p].astype(F32)
    second_ref[...] = second.T
    first = fown[b]
    for p in outer_peers:
        arrive(fbuf, f_rs, p, outer_dev(p))
        first = first + fbuf[p].astype(F32)
    first_ref[...] = first.T
    both = jnp.concatenate([first, second], axis=1).astype(BF16)
    for r in range(res):
        align_ref[:, r, :] = dot(both, wpad[r]).astype(BF16)
    for c in sends:
        c.wait_send()


def per_device(
    homolog_embedding,
    left_factor_matrix,
    right_factor_matrix,
    decoder,
    pair_output_bias,
    pair_output_gradient,
):
    rows, res, width = homolog_embedding.shape
    fac = left_factor_matrix.shape[1]
    chan = decoder.shape[1]
    count = lax.axis_size("col")
    inner = max(d for d in range(1, count + 1) if count % d == 0 and d * d <= count)
    outer = count // inner
    blk = res * fac
    ni = outer * res
    dma = pltpu.SemaphoreType.DMA
    first, second, align = pl.pallas_call(
        functools.partial(kernel, inner, outer),
        out_shape=[
            jax.ShapeDtypeStruct((blk, rows), F32),
            jax.ShapeDtypeStruct((blk, rows), F32),
            jax.ShapeDtypeStruct((rows, res, width), BF16),
        ],
        in_specs=[pl.BlockSpec(memory_space=pltpu.VMEM)] * 6,
        out_specs=[pl.BlockSpec(memory_space=pltpu.VMEM)] * 3,
        scratch_shapes=[
            pltpu.VMEM((outer, rows, blk), BF16),
            pltpu.VMEM((inner, rows, blk), BF16),
            pltpu.VMEM((inner, outer, res, res, chan), BF16),
            pltpu.VMEM((outer, rows, blk), F32),
            pltpu.VMEM((inner, rows, blk), F32),
            pltpu.VMEM((outer, rows, blk), BF16),
            pltpu.VMEM((inner, rows, blk), BF16),
            pltpu.VMEM((outer, rows, blk), BF16),
            pltpu.VMEM((inner, rows, blk), BF16),
            pltpu.VMEM((res, 2 * blk, width), BF16),
            pltpu.VMEM((fac * blk, res * chan), BF16),
            pltpu.VMEM((fac * ni, fac * ni), BF16),
            pltpu.VMEM((inner * ni, res * chan), F32),
            pltpu.VMEM((inner * ni, fac * blk), BF16),
            pltpu.VMEM((fac * ni, inner * blk), BF16),
            dma((outer,)),
            dma((outer,)),
            dma((inner,)),
            dma((inner,)),
            dma((inner,)),
            dma((inner,)),
            dma((outer,)),
            dma((outer,)),
            dma((inner,)),
            dma((inner,)),
            dma,
        ],
        compiler_params=pltpu.CompilerParams(collective_id=0, has_side_effects=True),
        name="pair_backward",
    )(
        homolog_embedding,
        left_factor_matrix.T,
        right_factor_matrix.T,
        decoder,
        pair_output_bias.reshape(1, chan),
        pair_output_gradient.reshape(outer, inner * res, res, chan),
    )
    first = first.reshape(res, fac, rows).transpose(2, 0, 1)
    second = second.reshape(res, fac, rows).transpose(2, 0, 1)
    return first, second, align


def solution(mesh):
    placed = (P("group", "col", None), P(), P(), P(), P(), P("group", "col", None))
    return jax.shard_map(
        per_device,
        mesh=mesh,
        in_specs=placed,
        out_specs=(P("group", "col", None), P("group", "col", None), P("group", "col", None)),
        check_vma=False,
    )
```

```python
import functools

import jax
import jax.numpy as jnp
from jax import lax
from jax.experimental import pallas as pl
from jax.experimental.pallas import tpu as pltpu
from jax.sharding import PartitionSpec as P

MESH = pl.DeviceIdType.MESH
F32 = jnp.float32
BF16 = jnp.bfloat16


def dot(x, y, dims=((1,), (0,))):
    return lax.dot_general(x, y, (dims, ((), ())), preferred_element_type=F32)


NT = ((1,), (1,))
TN = ((0,), (0,))


def exchange_lanes(parts, group):
    parts = list(parts)
    width = parts[0].shape[1]
    lane = lax.broadcasted_iota(jnp.int32, parts[0].shape, 1) // group
    step = len(parts) // 2
    while step:
        high = lax.rem(lane // step, 2) == 1
        for p in range(len(parts)):
            if p // step % 2 == 0:
                x, y = parts[p], parts[p + step]
                parts[p] = jnp.where(high, pltpu.roll(y, step * group, 1), x)
                parts[p + step] = jnp.where(high, y, pltpu.roll(x, width - step * group, 1))
        step //= 2
    return parts


def place_factors(wpad, wl, wr):
    res = wpad.shape[0]
    fac = wl.shape[0]
    wpad[...] = jnp.zeros_like(wpad)
    for r in range(res):
        wpad[r, r * fac : (r + 1) * fac, :] = wl
        wpad[r, (res + r) * fac : (res + r + 1) * fac, :] = wr


def kernel(
    inner,
    outer,
    e_hbm,
    wl_hbm,
    wr_hbm,
    dec_hbm,
    bias_hbm,
    g_hbm,
    both_ref,
    e_ref,
    wl_ref,
    wr_ref,
    dec_ref,
    bias_ref,
    lbuf,
    rbuf,
    gbuf,
    fown,
    sown,
    fsend,
    ssend,
    fbuf,
    sbuf,
    wpad,
    perm,
    gf,
    mt,
    s2,
    l_ss,
    l_rs,
    r_ss,
    r_rs,
    g_ss,
    g_rs,
    f_ss,
    f_rs,
    s_ss,
    s_rs,
    in_sem,
):
    rows, res, width = e_ref.shape
    fac = wl_ref.shape[0]
    chan = dec_ref.shape[1]
    blk = res * fac
    ni = outer * res
    recip = 1.0 / rows
    me = lax.axis_index("col")
    a = lax.rem(me, inner)
    b = me // inner

    inner_peers = [lax.rem(a + k, inner) for k in range(1, inner)]
    outer_peers = [lax.rem(b + k, outer) for k in range(1, outer)]

    def inner_dev(p):
        return {"col": b * inner + p}

    def outer_dev(p):
        return {"col": p * inner + a}

    barrier = pltpu.get_barrier_semaphore()
    for p in outer_peers:
        pl.semaphore_signal(barrier, inc=1, device_id=outer_dev(p), device_id_type=MESH)
    for p in inner_peers:
        pl.semaphore_signal(barrier, inc=1, device_id=inner_dev(p), device_id_type=MESH)

    loads = []
    for k, (src, dst) in enumerate(
        [
            (wl_hbm, wl_ref),
            (wr_hbm, wr_ref),
            (e_hbm, e_ref),
            (g_hbm.at[:, pl.ds(a * res, res)], gbuf.at[a]),
            (dec_hbm, dec_ref),
            (bias_hbm, bias_ref),
        ]
    ):
        c = pltpu.make_async_copy(src, dst, in_sem.at[k])
        c.start()
        loads.append(c)

    loads[0].wait()
    loads[1].wait()
    place_factors(wpad, wl_ref[...], wr_ref[...])

    def send(src, dst, ss, rs, dev):
        c = pltpu.make_async_remote_copy(
            src_ref=src, dst_ref=dst, send_sem=ss, recv_sem=rs, device_id=dev, device_id_type=MESH
        )
        c.start()
        return c

    def arrive(buf, rs, p, dev):
        pltpu.make_async_remote_copy(
            src_ref=buf.at[p],
            dst_ref=buf.at[p],
            send_sem=rs.at[p],
            recv_sem=rs.at[p],
            device_id=dev,
            device_id_type=MESH,
        ).wait_recv()

    loads[2].wait()
    pl.semaphore_wait(barrier, inner + outer - 2)
    sends = []
    for k, p in enumerate(inner_peers):
        sends.append(
            send(
                g_hbm.at[:, pl.ds(p * res, res)], gbuf.at[a], g_ss.at[k], g_rs.at[a], inner_dev(p)
            )
        )
    acc = dot(e_ref[:, 0, :], wpad[0], NT)
    for r in range(1, res):
        acc = acc + dot(e_ref[:, r, :], wpad[r], NT)
    acc = acc.astype(BF16)
    lbuf[b] = acc[:, :blk]
    for k, p in enumerate(outer_peers):
        sends.append(send(lbuf.at[b], lbuf.at[b], l_ss.at[k], l_rs.at[b], outer_dev(p)))
    rbuf[a] = acc[:, blk:]
    for k, p in enumerate(inner_peers):
        sends.append(send(rbuf.at[a], rbuf.at[a], r_ss.at[k], r_rs.at[a], inner_dev(p)))

    out_pos = lax.broadcasted_iota(jnp.int32, perm.shape, 0)
    in_pos = lax.broadcasted_iota(jnp.int32, perm.shape, 1)
    hit = in_pos == lax.rem(out_pos, ni) * fac + out_pos // ni
    perm[...] = jnp.where(hit, 1.0, 0.0).astype(BF16)
    loads[3].wait()
    loads[4].wait()
    loads[5].wait()
    for p in inner_peers:
        arrive(gbuf, g_rs, p, inner_dev(p))
    span = inner * ni
    for q in range(inner):
        up = gbuf[q].reshape(ni, res, chan).astype(F32) * 2.0
        for r in range(res):
            gf[r * span + q * ni : r * span + (q + 1) * ni, :] = up[:, r, :]

    for p in outer_peers:
        arrive(lbuf, l_rs, p, outer_dev(p))
    left = jnp.concatenate([lbuf[q] for q in range(outer)], axis=1)
    left_p = dot(left, perm[...], NT).astype(BF16)

    for p in inner_peers:
        arrive(rbuf, r_rs, p, inner_dev(p))
    right = jnp.concatenate([rbuf[q] for q in range(inner)], axis=1)
    prod = (dot(left_p, right, TN) * recip).astype(BF16)
    for cg in range(fac // res):
        for q in range(inner):
            parts = [
                prod[c * ni : (c + 1) * ni, q * blk : (q + 1) * blk]
                for c in range(cg * res, (cg + 1) * res)
            ]
            for r, part in enumerate(exchange_lanes(parts, fac)):
                mt[r * span + q * ni : r * span + (q + 1) * ni, cg * blk : (cg + 1) * blk] = (
                    part.astype(BF16)
                )
    linear = dot(mt[...], dec_ref[...]) + bias_ref[...]
    pre = (gf[...] * jnp.maximum(linear, 0.0)).astype(BF16)
    slopes = (dot(pre, dec_ref[...], NT) * recip).astype(BF16)
    for cg in range(fac // res):
        for q in range(inner):
            parts = [
                slopes[r * span + q * ni : r * span + (q + 1) * ni, cg * blk : (cg + 1) * blk]
                for r in range(res)
            ]
            for k, part in enumerate(exchange_lanes(parts, fac)):
                c = cg * res + k
                s2[c * ni : (c + 1) * ni, q * blk : (q + 1) * blk] = part.astype(BF16)

    first_part = dot(right, s2[...], NT).astype(BF16)
    first_part = dot(first_part, perm[...])
    for q in range(outer):
        term = first_part[:, q * blk : (q + 1) * blk]
        fown[q] = term
        fsend[q] = term.astype(BF16)
    for k, p in enumerate(outer_peers):
        sends.append(send(fsend.at[p], fbuf.at[b], f_ss.at[k], f_rs.at[b], outer_dev(p)))
    second_part = dot(left_p, s2[...])
    for q in range(inner):
        term = second_part[:, q * blk : (q + 1) * blk]
        sown[q] = term
        ssend[q] = term.astype(BF16)
    for k, p in enumerate(inner_peers):
        sends.append(send(ssend.at[p], sbuf.at[a], s_ss.at[k], s_rs.at[a], inner_dev(p)))

    second = sown[a]
    for p in inner_peers:
        arrive(sbuf, s_rs, p, inner_dev(p))
        second = second + sbuf[p].astype(F32)
    both_ref[:, blk:] = second
    first = fown[b]
    for p in outer_peers:
        arrive(fbuf, f_rs, p, outer_dev(p))
        first = first + fbuf[p].astype(F32)
    both_ref[:, :blk] = first
    for c in sends:
        c.wait_send()


def finish(both_ref, wl_ref, wr_ref, first_ref, second_ref, align_ref, wpad):
    place_factors(wpad, wl_ref[...], wr_ref[...])
    both = both_ref[...]
    blk = both.shape[1] // 2
    first_ref[...] = both[:, :blk].T
    second_ref[...] = both[:, blk:].T
    both = both.astype(BF16)
    for r in range(align_ref.shape[1]):
        align_ref[:, r, :] = dot(both, wpad[r]).astype(BF16)


def per_device(
    homolog_embedding,
    left_factor_matrix,
    right_factor_matrix,
    decoder,
    pair_output_bias,
    pair_output_gradient,
):
    rows, res, width = homolog_embedding.shape
    fac = left_factor_matrix.shape[1]
    chan = decoder.shape[1]
    count = lax.axis_size("col")
    inner = max(d for d in range(1, count + 1) if count % d == 0 and d * d <= count)
    outer = count // inner
    blk = res * fac
    ni = outer * res
    dma = pltpu.SemaphoreType.DMA
    vmem = pl.BlockSpec(memory_space=pltpu.VMEM)
    left_t = left_factor_matrix.T
    right_t = right_factor_matrix.T
    both = pl.pallas_call(
        functools.partial(kernel, inner, outer),
        out_shape=jax.ShapeDtypeStruct((rows, 2 * blk), F32),
        in_specs=[pl.BlockSpec(memory_space=pl.ANY)] * 6,
        out_specs=vmem,
        scratch_shapes=[
            pltpu.VMEM((rows, res, width), BF16),
            pltpu.VMEM((fac, width), BF16),
            pltpu.VMEM((fac, width), BF16),
            pltpu.VMEM(decoder.shape, BF16),
            pltpu.VMEM((1, chan), F32),
            pltpu.VMEM((outer, rows, blk), BF16),
            pltpu.VMEM((inner, rows, blk), BF16),
            pltpu.VMEM((inner, outer, res, res, chan), BF16),
            pltpu.VMEM((outer, rows, blk), F32),
            pltpu.VMEM((inner, rows, blk), F32),
            pltpu.VMEM((outer, rows, blk), BF16),
            pltpu.VMEM((inner, rows, blk), BF16),
            pltpu.VMEM((outer, rows, blk), BF16),
            pltpu.VMEM((inner, rows, blk), BF16),
            pltpu.VMEM((res, 2 * blk, width), BF16),
            pltpu.VMEM((fac * ni, fac * ni), BF16),
            pltpu.VMEM((res * inner * ni, chan), F32),
            pltpu.VMEM((res * inner * ni, fac * fac), BF16),
            pltpu.VMEM((fac * ni, inner * blk), BF16),
            dma((outer,)),
            dma((outer,)),
            dma((inner,)),
            dma((inner,)),
            dma((inner,)),
            dma((inner,)),
            dma((outer,)),
            dma((outer,)),
            dma((inner,)),
            dma((inner,)),
            dma((6,)),
        ],
        compiler_params=pltpu.CompilerParams(collective_id=0, has_side_effects=True),
        name="pair_backward",
    )(
        homolog_embedding,
        left_t,
        right_t,
        decoder,
        pair_output_bias.reshape(1, chan),
        pair_output_gradient.reshape(outer, inner * res, res, chan),
    )
    first, second, align = pl.pallas_call(
        finish,
        out_shape=[
            jax.ShapeDtypeStruct((blk, rows), F32),
            jax.ShapeDtypeStruct((blk, rows), F32),
            jax.ShapeDtypeStruct((rows, res, width), BF16),
        ],
        in_specs=[vmem] * 3,
        out_specs=[vmem] * 3,
        scratch_shapes=[pltpu.VMEM((res, 2 * blk, width), BF16)],
        name="finish",
    )(both, left_t, right_t)
    first = first.reshape(res, fac, rows).transpose(2, 0, 1)
    second = second.reshape(res, fac, rows).transpose(2, 0, 1)
    return first, second, align


def solution(mesh):
    placed = (P("group", "col", None), P(), P(), P(), P(), P("group", "col", None))
    return jax.shard_map(
        per_device,
        mesh=mesh,
        in_specs=placed,
        out_specs=(P("group", "col", None), P("group", "col", None), P("group", "col", None)),
        check_vma=False,
    )
```

```python
import functools

import jax
import jax.numpy as jnp
from jax import lax
from jax.experimental import pallas as pl
from jax.experimental.pallas import tpu as pltpu
from jax.sharding import PartitionSpec as P

MESH = pl.DeviceIdType.MESH
F32 = jnp.float32
BF16 = jnp.bfloat16


def dot(x, y, dims=((1,), (0,))):
    return lax.dot_general(x, y, (dims, ((), ())), preferred_element_type=F32)


NT = ((1,), (1,))
TN = ((0,), (0,))


def place_factors(wpad, wl, wr):
    res = wpad.shape[0]
    fac = wl.shape[0]
    wpad[...] = jnp.zeros_like(wpad)
    for r in range(res):
        wpad[r, r * fac : (r + 1) * fac, :] = wl
        wpad[r, (res + r) * fac : (res + r + 1) * fac, :] = wr


def kernel(
    inner,
    outer,
    e_hbm,
    wl_hbm,
    wr_hbm,
    dec_hbm,
    bias_hbm,
    g_hbm,
    both_ref,
    e_ref,
    wl_ref,
    wr_ref,
    dec_ref,
    bias_ref,
    lbuf,
    rbuf,
    gbuf,
    fown,
    sown,
    fsend,
    ssend,
    fbuf,
    sbuf,
    wtile,
    mask,
    pick,
    perm,
    swap,
    gf,
    mt,
    s2,
    l_ss,
    l_rs,
    r_ss,
    r_rs,
    g_ss,
    g_rs,
    f_ss,
    f_rs,
    s_ss,
    s_rs,
    in_sem,
):
    rows, res, width = e_ref.shape
    fac = wl_ref.shape[0]
    chan = dec_ref.shape[1]
    blk = res * fac
    ni = outer * res
    recip = 1.0 / rows
    me = lax.axis_index("col")
    a = lax.rem(me, inner)
    b = me // inner

    inner_peers = [lax.rem(a + k, inner) for k in range(1, inner)]
    outer_peers = []
    for k in range(outer - 1):
        low = outer - 1 - k
        low = jnp.where(low > b, low, low - 1)
        high = jnp.where(k < b, k, k + 1)
        outer_peers.append(jnp.where(2 * b < outer, low, high))

    def inner_dev(p):
        return {"col": b * inner + p}

    def outer_dev(p):
        return {"col": p * inner + a}

    barrier = pltpu.get_barrier_semaphore()
    for p in outer_peers:
        pl.semaphore_signal(barrier, inc=1, device_id=outer_dev(p), device_id_type=MESH)
    for p in inner_peers:
        pl.semaphore_signal(barrier, inc=1, device_id=inner_dev(p), device_id_type=MESH)

    loads = []
    for k, (src, dst) in enumerate(
        [
            (wl_hbm, wl_ref),
            (wr_hbm, wr_ref),
            (e_hbm, e_ref),
            (g_hbm.at[:, pl.ds(a * res, res)], gbuf.at[a]),
            (dec_hbm, dec_ref),
            (bias_hbm, bias_ref),
        ]
    ):
        c = pltpu.make_async_copy(src, dst, in_sem.at[k])
        c.start()
        loads.append(c)

    row_pos = lax.broadcasted_iota(jnp.int32, mask.shape, 0)
    lane_pos = lax.broadcasted_iota(jnp.int32, mask.shape, 1)
    mask[...] = jnp.where(lax.rem(row_pos, res) == lax.rem(lane_pos // fac, res), 1.0, 0.0)
    row_pos = lax.broadcasted_iota(jnp.int32, pick.shape, 0)
    lane_pos = lax.broadcasted_iota(jnp.int32, pick.shape, 1)
    pick[...] = jnp.where(lane_pos // res == row_pos, 1.0, 0.0).astype(BF16)

    loads[0].wait()
    loads[1].wait()
    for r in range(res):
        wtile[r * fac : (r + 1) * fac, :] = wl_ref[...]
        wtile[(res + r) * fac : (res + r + 1) * fac, :] = wr_ref[...]

    def send(src, dst, ss, rs, dev):
        c = pltpu.make_async_remote_copy(
            src_ref=src, dst_ref=dst, send_sem=ss, recv_sem=rs, device_id=dev, device_id_type=MESH
        )
        c.start()
        return c

    def arrive(buf, rs, p, dev):
        pltpu.make_async_remote_copy(
            src_ref=buf.at[p],
            dst_ref=buf.at[p],
            send_sem=rs.at[p],
            recv_sem=rs.at[p],
            device_id=dev,
            device_id_type=MESH,
        ).wait_recv()

    loads[2].wait()
    pl.semaphore_wait(barrier, inner + outer - 2)
    sends = []
    for k, p in enumerate(inner_peers):
        sends.append(
            send(
                g_hbm.at[:, pl.ds(p * res, res)], gbuf.at[a], g_ss.at[k], g_rs.at[a], inner_dev(p)
            )
        )
    flat = dot(e_ref[...].reshape(rows * res, width), wtile[...], NT)
    flat = jnp.where(mask[...] > 0.0, flat, 0.0)
    acc = dot(pick[...], flat.astype(BF16)).astype(BF16)
    lbuf[b] = acc[:, :blk]
    for k, p in enumerate(outer_peers):
        sends.append(send(lbuf.at[b], lbuf.at[b], l_ss.at[k], l_rs.at[b], outer_dev(p)))
    rbuf[a] = acc[:, blk:]
    for k, p in enumerate(inner_peers):
        sends.append(send(rbuf.at[a], rbuf.at[a], r_ss.at[k], r_rs.at[a], inner_dev(p)))

    out_pos = lax.broadcasted_iota(jnp.int32, perm.shape, 0)
    in_pos = lax.broadcasted_iota(jnp.int32, perm.shape, 1)
    hit = in_pos == lax.rem(out_pos, ni) * fac + out_pos // ni
    perm[...] = jnp.where(hit, 1.0, 0.0).astype(BF16)
    out_pos = lax.broadcasted_iota(jnp.int32, swap.shape, 0)
    in_pos = lax.broadcasted_iota(jnp.int32, swap.shape, 1)
    hit = (
        (out_pos // blk == lax.rem(in_pos // fac, res))
        & (in_pos // blk == lax.rem(out_pos // fac, res))
        & (lax.rem(out_pos, fac) == lax.rem(in_pos, fac))
    )
    swap[...] = jnp.where(hit, 1.0, 0.0).astype(BF16)
    loads[3].wait()
    loads[4].wait()
    loads[5].wait()
    for p in inner_peers:
        arrive(gbuf, g_rs, p, inner_dev(p))
    span = inner * ni
    for q in range(inner):
        up = gbuf[q].reshape(ni, res, chan).astype(F32) * 2.0
        for r in range(res):
            gf[r * span + q * ni : r * span + (q + 1) * ni, :] = up[:, r, :]

    for p in outer_peers:
        arrive(lbuf, l_rs, p, outer_dev(p))
    left = jnp.concatenate([lbuf[q] for q in range(outer)], axis=1)
    left_p = dot(left, perm[...], NT).astype(BF16)

    for p in inner_peers:
        arrive(rbuf, r_rs, p, inner_dev(p))
    right = jnp.concatenate([rbuf[q] for q in range(inner)], axis=1)
    prod = (dot(left_p, right, TN) * recip).astype(BF16)
    groups = [(cg, q) for cg in range(fac // res) for q in range(inner)]
    mixed = jnp.concatenate(
        [
            jnp.concatenate(
                [
                    prod[(cg * res + k) * ni : (cg * res + k + 1) * ni, q * blk : (q + 1) * blk]
                    for cg, q in groups
                ],
                axis=0,
            )
            for k in range(res)
        ],
        axis=1,
    )
    mixed = dot(mixed, swap[...]).astype(BF16)
    for n, (cg, q) in enumerate(groups):
        for r in range(res):
            mt[r * span + q * ni : r * span + (q + 1) * ni, cg * blk : (cg + 1) * blk] = mixed[
                n * ni : (n + 1) * ni, r * blk : (r + 1) * blk
            ]
    linear = dot(mt[...], dec_ref[...]) + bias_ref[...]
    pre = (gf[...] * jnp.maximum(linear, 0.0)).astype(BF16)
    slopes = (dot(pre, dec_ref[...], NT) * recip).astype(BF16)
    mixed = jnp.concatenate(
        [
            jnp.concatenate(
                [
                    slopes[r * span + q * ni : r * span + (q + 1) * ni, cg * blk : (cg + 1) * blk]
                    for cg, q in groups
                ],
                axis=0,
            )
            for r in range(res)
        ],
        axis=1,
    )
    mixed = dot(mixed, swap[...]).astype(BF16)
    for n, (cg, q) in enumerate(groups):
        for k in range(res):
            c = cg * res + k
            s2[c * ni : (c + 1) * ni, q * blk : (q + 1) * blk] = mixed[
                n * ni : (n + 1) * ni, k * blk : (k + 1) * blk
            ]

    first_part = dot(right, s2[...], NT).astype(BF16)
    first_part = dot(first_part, perm[...])
    for q in range(outer):
        term = first_part[:, q * blk : (q + 1) * blk]
        fown[q] = term
        fsend[q] = term.astype(BF16)
    for k, p in enumerate(outer_peers):
        sends.append(send(fsend.at[p], fbuf.at[b], f_ss.at[k], f_rs.at[b], outer_dev(p)))
    second_part = dot(left_p, s2[...])
    for q in range(inner):
        term = second_part[:, q * blk : (q + 1) * blk]
        sown[q] = term
        ssend[q] = term.astype(BF16)
    for k, p in enumerate(inner_peers):
        sends.append(send(ssend.at[p], sbuf.at[a], s_ss.at[k], s_rs.at[a], inner_dev(p)))

    second = sown[a]
    for p in inner_peers:
        arrive(sbuf, s_rs, p, inner_dev(p))
        second = second + sbuf[p].astype(F32)
    both_ref[:, blk:] = second
    first = fown[b]
    for p in outer_peers:
        arrive(fbuf, f_rs, p, outer_dev(p))
        first = first + fbuf[p].astype(F32)
    both_ref[:, :blk] = first
    for c in sends:
        c.wait_send()


def finish(both_ref, wl_ref, wr_ref, first_ref, second_ref, align_ref, wpad):
    place_factors(wpad, wl_ref[...], wr_ref[...])
    both = both_ref[...]
    blk = both.shape[1] // 2
    first_ref[...] = both[:, :blk].T
    second_ref[...] = both[:, blk:].T
    both = both.astype(BF16)
    for r in range(align_ref.shape[1]):
        align_ref[:, r, :] = dot(both, wpad[r]).astype(BF16)


def per_device(
    homolog_embedding,
    left_factor_matrix,
    right_factor_matrix,
    decoder,
    pair_output_bias,
    pair_output_gradient,
):
    rows, res, width = homolog_embedding.shape
    fac = left_factor_matrix.shape[1]
    chan = decoder.shape[1]
    count = lax.axis_size("col")
    inner = max(d for d in range(1, count + 1) if count % d == 0 and d * d <= count)
    outer = count // inner
    blk = res * fac
    ni = outer * res
    dma = pltpu.SemaphoreType.DMA
    vmem = pl.BlockSpec(memory_space=pltpu.VMEM)
    left_t = left_factor_matrix.T
    right_t = right_factor_matrix.T
    both = pl.pallas_call(
        functools.partial(kernel, inner, outer),
        out_shape=jax.ShapeDtypeStruct((rows, 2 * blk), F32),
        in_specs=[pl.BlockSpec(memory_space=pltpu.HBM)] * 6,
        out_specs=vmem,
        scratch_shapes=[
            pltpu.VMEM((rows, res, width), BF16),
            pltpu.VMEM((fac, width), BF16),
            pltpu.VMEM((fac, width), BF16),
            pltpu.VMEM(decoder.shape, BF16),
            pltpu.VMEM((1, chan), F32),
            pltpu.VMEM((outer, rows, blk), BF16),
            pltpu.VMEM((inner, rows, blk), BF16),
            pltpu.VMEM((inner, outer, res, res, chan), BF16),
            pltpu.VMEM((outer, rows, blk), F32),
            pltpu.VMEM((inner, rows, blk), F32),
            pltpu.VMEM((outer, rows, blk), BF16),
            pltpu.VMEM((inner, rows, blk), BF16),
            pltpu.VMEM((outer, rows, blk), BF16),
            pltpu.VMEM((inner, rows, blk), BF16),
            pltpu.VMEM((2 * blk, width), BF16),
            pltpu.VMEM((rows * res, 2 * blk), F32),
            pltpu.VMEM((rows, rows * res), BF16),
            pltpu.VMEM((fac * ni, fac * ni), BF16),
            pltpu.VMEM((res * blk, res * blk), BF16),
            pltpu.VMEM((res * inner * ni, chan), F32),
            pltpu.VMEM((res * inner * ni, fac * fac), BF16),
            pltpu.VMEM((fac * ni, inner * blk), BF16),
            dma((outer,)),
            dma((outer,)),
            dma((inner,)),
            dma((inner,)),
            dma((inner,)),
            dma((inner,)),
            dma((outer,)),
            dma((outer,)),
            dma((inner,)),
            dma((inner,)),
            dma((6,)),
        ],
        compiler_params=pltpu.CompilerParams(collective_id=0, has_side_effects=True, vmem_limit_bytes=24 * 1024 * 1024),
        name="pair_backward",
    )(
        *[
            pltpu.with_memory_space_constraint(x, pltpu.HBM)
            for x in (
                homolog_embedding,
                left_t,
                right_t,
                decoder,
                pair_output_bias.reshape(1, chan),
                pair_output_gradient.reshape(outer, inner * res, res, chan),
            )
        ]
    )
    first, second, align = pl.pallas_call(
        finish,
        out_shape=[
            jax.ShapeDtypeStruct((blk, rows), F32),
            jax.ShapeDtypeStruct((blk, rows), F32),
            jax.ShapeDtypeStruct((rows, res, width), BF16),
        ],
        in_specs=[vmem] * 3,
        out_specs=[vmem] * 3,
        scratch_shapes=[pltpu.VMEM((res, 2 * blk, width), BF16)],
        compiler_params=pltpu.CompilerParams(vmem_limit_bytes=16 * 1024 * 1024),
        name="finish",
    )(both, left_t, right_t)
    first = first.reshape(res, fac, rows).transpose(2, 0, 1)
    second = second.reshape(res, fac, rows).transpose(2, 0, 1)
    return first, second, align


def solution(mesh):
    placed = (P("group", "col", None), P(), P(), P(), P(), P("group", "col", None))
    return jax.shard_map(
        per_device,
        mesh=mesh,
        in_specs=placed,
        out_specs=(P("group", "col", None), P("group", "col", None), P("group", "col", None)),
        check_vma=False,
    )
```

```python
import functools

import jax
import jax.numpy as jnp
from jax import lax
from jax.experimental import pallas as pl
from jax.experimental.pallas import tpu as pltpu
from jax.sharding import PartitionSpec as P

MESH = pl.DeviceIdType.MESH
F32 = jnp.float32
BF16 = jnp.bfloat16


def dot(x, y, dims=((1,), (0,))):
    return lax.dot_general(x, y, (dims, ((), ())), preferred_element_type=F32)


NT = ((1,), (1,))
TN = ((0,), (0,))


def place_factors(wpad, wl, wr):
    res = wpad.shape[0]
    fac = wl.shape[0]
    wpad[...] = jnp.zeros_like(wpad)
    for r in range(res):
        wpad[r, r * fac : (r + 1) * fac, :] = wl
        wpad[r, (res + r) * fac : (res + r + 1) * fac, :] = wr


def kernel(
    inner,
    outer,
    e_hbm,
    wl_hbm,
    wr_hbm,
    dec_hbm,
    bias_hbm,
    g_hbm,
    both_ref,
    e_ref,
    wl_ref,
    wr_ref,
    dec_ref,
    bias_ref,
    lbuf,
    rbuf,
    gbuf,
    fown,
    sown,
    fsend,
    ssend,
    fbuf,
    sbuf,
    wtile,
    mask,
    pick,
    perm,
    swap,
    gf,
    mt,
    s2,
    l_ss,
    l_rs,
    r_ss,
    r_rs,
    g_ss,
    g_rs,
    f_ss,
    f_rs,
    s_ss,
    s_rs,
    in_sem,
):
    rows, res, width = e_ref.shape
    fac = wl_ref.shape[0]
    chan = dec_ref.shape[1]
    blk = res * fac
    ni = outer * res
    recip = 1.0 / rows
    me = lax.axis_index("col")
    a = lax.rem(me, inner)
    b = me // inner

    inner_peers = [lax.rem(a + k, inner) for k in range(1, inner)]
    outer_peers = []
    for k in range(outer - 1):
        low = outer - 1 - k
        low = jnp.where(low > b, low, low - 1)
        high = jnp.where(k < b, k, k + 1)
        outer_peers.append(jnp.where(2 * b < outer, low, high))

    def inner_dev(p):
        return {"col": b * inner + p}

    def outer_dev(p):
        return {"col": p * inner + a}

    barrier = pltpu.get_barrier_semaphore()
    for p in outer_peers:
        pl.semaphore_signal(barrier, inc=1, device_id=outer_dev(p), device_id_type=MESH)
    for p in inner_peers:
        pl.semaphore_signal(barrier, inc=1, device_id=inner_dev(p), device_id_type=MESH)

    loads = []
    for k, (src, dst) in enumerate(
        [
            (wl_hbm, wl_ref),
            (wr_hbm, wr_ref),
            (e_hbm, e_ref),
            (g_hbm.at[:, pl.ds(a * res, res)], gbuf.at[a]),
            (dec_hbm, dec_ref),
            (bias_hbm, bias_ref),
        ]
    ):
        c = pltpu.make_async_copy(src, dst, in_sem.at[k])
        c.start()
        loads.append(c)

    row_pos = lax.broadcasted_iota(jnp.int32, mask.shape, 0)
    lane_pos = lax.broadcasted_iota(jnp.int32, mask.shape, 1)
    mask[...] = jnp.where(lax.rem(row_pos, res) == lax.rem(lane_pos // fac, res), 1.0, 0.0)
    row_pos = lax.broadcasted_iota(jnp.int32, pick.shape, 0)
    lane_pos = lax.broadcasted_iota(jnp.int32, pick.shape, 1)
    pick[...] = jnp.where(lane_pos // res == row_pos, 1.0, 0.0).astype(BF16)

    loads[0].wait()
    loads[1].wait()
    for r in range(res):
        wtile[r * fac : (r + 1) * fac, :] = wl_ref[...]
        wtile[(res + r) * fac : (res + r + 1) * fac, :] = wr_ref[...]

    def send(src, dst, ss, rs, dev):
        c = pltpu.make_async_remote_copy(
            src_ref=src, dst_ref=dst, send_sem=ss, recv_sem=rs, device_id=dev, device_id_type=MESH
        )
        c.start()
        return c

    def arrive(buf, rs, p, dev):
        pltpu.make_async_remote_copy(
            src_ref=buf.at[p],
            dst_ref=buf.at[p],
            send_sem=rs.at[p],
            recv_sem=rs.at[p],
            device_id=dev,
            device_id_type=MESH,
        ).wait_recv()

    loads[2].wait()
    sends = []
    flat = dot(e_ref[...].reshape(rows * res, width), wtile[...], NT)
    flat = jnp.where(mask[...] > 0.0, flat, 0.0)
    acc = dot(pick[...], flat.astype(BF16)).astype(BF16)
    lbuf[b] = acc[:, :blk]
    pl.semaphore_wait(barrier, inner + outer - 2)
    for k, p in enumerate(outer_peers):
        sends.append(send(lbuf.at[b], lbuf.at[b], l_ss.at[k], l_rs.at[b], outer_dev(p)))
    rbuf[a] = acc[:, blk:]
    for k, p in enumerate(inner_peers):
        sends.append(send(rbuf.at[a], rbuf.at[a], r_ss.at[k], r_rs.at[a], inner_dev(p)))

    for k, p in enumerate(inner_peers):
        sends.append(
            send(
                g_hbm.at[:, pl.ds(p * res, res)], gbuf.at[a], g_ss.at[k], g_rs.at[a], inner_dev(p)
            )
        )
    out_pos = lax.broadcasted_iota(jnp.int32, perm.shape, 0)
    in_pos = lax.broadcasted_iota(jnp.int32, perm.shape, 1)
    hit = in_pos == lax.rem(out_pos, ni) * fac + out_pos // ni
    perm[...] = jnp.where(hit, 1.0, 0.0).astype(BF16)
    out_pos = lax.broadcasted_iota(jnp.int32, swap.shape, 0)
    in_pos = lax.broadcasted_iota(jnp.int32, swap.shape, 1)
    hit = (
        (out_pos // blk == lax.rem(in_pos // fac, res))
        & (in_pos // blk == lax.rem(out_pos // fac, res))
        & (lax.rem(out_pos, fac) == lax.rem(in_pos, fac))
    )
    swap[...] = jnp.where(hit, 1.0, 0.0).astype(BF16)
    loads[3].wait()
    loads[4].wait()
    loads[5].wait()
    for p in inner_peers:
        arrive(gbuf, g_rs, p, inner_dev(p))
    span = inner * ni
    for q in range(inner):
        up = gbuf[q].reshape(ni, res, chan).astype(F32) * 2.0
        for r in range(res):
            gf[r * span + q * ni : r * span + (q + 1) * ni, :] = up[:, r, :]

    for p in outer_peers:
        arrive(lbuf, l_rs, p, outer_dev(p))
    left = jnp.concatenate([lbuf[q] for q in range(outer)], axis=1)
    left_p = dot(left, perm[...], NT).astype(BF16)

    for p in inner_peers:
        arrive(rbuf, r_rs, p, inner_dev(p))
    right = jnp.concatenate([rbuf[q] for q in range(inner)], axis=1)
    prod = (dot(left_p, right, TN) * recip).astype(BF16)
    groups = [(cg, q) for cg in range(fac // res) for q in range(inner)]
    mixed = jnp.concatenate(
        [
            jnp.concatenate(
                [
                    prod[(cg * res + k) * ni : (cg * res + k + 1) * ni, q * blk : (q + 1) * blk]
                    for cg, q in groups
                ],
                axis=0,
            )
            for k in range(res)
        ],
        axis=1,
    )
    mixed = dot(mixed, swap[...]).astype(BF16)
    for n, (cg, q) in enumerate(groups):
        for r in range(res):
            mt[r * span + q * ni : r * span + (q + 1) * ni, cg * blk : (cg + 1) * blk] = mixed[
                n * ni : (n + 1) * ni, r * blk : (r + 1) * blk
            ]
    linear = dot(mt[...], dec_ref[...]) + bias_ref[...]
    pre = (gf[...] * jnp.maximum(linear, 0.0)).astype(BF16)
    slopes = (dot(pre, dec_ref[...], NT) * recip).astype(BF16)
    mixed = jnp.concatenate(
        [
            jnp.concatenate(
                [
                    slopes[r * span + q * ni : r * span + (q + 1) * ni, cg * blk : (cg + 1) * blk]
                    for cg, q in groups
                ],
                axis=0,
            )
            for r in range(res)
        ],
        axis=1,
    )
    mixed = dot(mixed, swap[...]).astype(BF16)
    for n, (cg, q) in enumerate(groups):
        for k in range(res):
            c = cg * res + k
            s2[c * ni : (c + 1) * ni, q * blk : (q + 1) * blk] = mixed[
                n * ni : (n + 1) * ni, k * blk : (k + 1) * blk
            ]

    first_part = dot(right, s2[...], NT).astype(BF16)
    first_part = dot(first_part, perm[...])
    for q in range(outer):
        term = first_part[:, q * blk : (q + 1) * blk]
        fown[q] = term
        fsend[q] = term.astype(BF16)
    for k, p in enumerate(outer_peers):
        sends.append(send(fsend.at[p], fbuf.at[b], f_ss.at[k], f_rs.at[b], outer_dev(p)))
    second_part = dot(left_p, s2[...])
    for q in range(inner):
        term = second_part[:, q * blk : (q + 1) * blk]
        sown[q] = term
        ssend[q] = term.astype(BF16)
    for k, p in enumerate(inner_peers):
        sends.append(send(ssend.at[p], sbuf.at[a], s_ss.at[k], s_rs.at[a], inner_dev(p)))

    second = sown[a]
    for p in inner_peers:
        arrive(sbuf, s_rs, p, inner_dev(p))
        second = second + sbuf[p].astype(F32)
    both_ref[:, blk:] = second
    first = fown[b]
    for p in outer_peers:
        arrive(fbuf, f_rs, p, outer_dev(p))
        first = first + fbuf[p].astype(F32)
    both_ref[:, :blk] = first
    for c in sends:
        c.wait_send()


def finish(both_ref, wl_ref, wr_ref, first_ref, second_ref, align_ref, wpad):
    place_factors(wpad, wl_ref[...], wr_ref[...])
    both = both_ref[...]
    blk = both.shape[1] // 2
    first_ref[...] = both[:, :blk].T
    second_ref[...] = both[:, blk:].T
    both = both.astype(BF16)
    for r in range(align_ref.shape[1]):
        align_ref[:, r, :] = dot(both, wpad[r]).astype(BF16)


def per_device(
    homolog_embedding,
    left_factor_matrix,
    right_factor_matrix,
    decoder,
    pair_output_bias,
    pair_output_gradient,
):
    rows, res, width = homolog_embedding.shape
    fac = left_factor_matrix.shape[1]
    chan = decoder.shape[1]
    count = lax.axis_size("col")
    inner = max(d for d in range(1, count + 1) if count % d == 0 and d * d <= count)
    outer = count // inner
    blk = res * fac
    ni = outer * res
    dma = pltpu.SemaphoreType.DMA
    vmem = pl.BlockSpec(memory_space=pltpu.VMEM)
    left_t = left_factor_matrix.T
    right_t = right_factor_matrix.T
    both = pl.pallas_call(
        functools.partial(kernel, inner, outer),
        out_shape=jax.ShapeDtypeStruct((rows, 2 * blk), F32),
        in_specs=[pl.BlockSpec(memory_space=pltpu.HBM)] * 6,
        out_specs=vmem,
        scratch_shapes=[
            pltpu.VMEM((rows, res, width), BF16),
            pltpu.VMEM((fac, width), BF16),
            pltpu.VMEM((fac, width), BF16),
            pltpu.VMEM(decoder.shape, BF16),
            pltpu.VMEM((1, chan), F32),
            pltpu.VMEM((outer, rows, blk), BF16),
            pltpu.VMEM((inner, rows, blk), BF16),
            pltpu.VMEM((inner, outer, res, res, chan), BF16),
            pltpu.VMEM((outer, rows, blk), F32),
            pltpu.VMEM((inner, rows, blk), F32),
            pltpu.VMEM((outer, rows, blk), BF16),
            pltpu.VMEM((inner, rows, blk), BF16),
            pltpu.VMEM((outer, rows, blk), BF16),
            pltpu.VMEM((inner, rows, blk), BF16),
            pltpu.VMEM((2 * blk, width), BF16),
            pltpu.VMEM((rows * res, 2 * blk), F32),
            pltpu.VMEM((rows, rows * res), BF16),
            pltpu.VMEM((fac * ni, fac * ni), BF16),
            pltpu.VMEM((res * blk, res * blk), BF16),
            pltpu.VMEM((res * inner * ni, chan), F32),
            pltpu.VMEM((res * inner * ni, fac * fac), BF16),
            pltpu.VMEM((fac * ni, inner * blk), BF16),
            dma((outer,)),
            dma((outer,)),
            dma((inner,)),
            dma((inner,)),
            dma((inner,)),
            dma((inner,)),
            dma((outer,)),
            dma((outer,)),
            dma((inner,)),
            dma((inner,)),
            dma((6,)),
        ],
        compiler_params=pltpu.CompilerParams(collective_id=0, has_side_effects=True, vmem_limit_bytes=24 * 1024 * 1024),
        name="pair_backward",
    )(
        *[
            pltpu.with_memory_space_constraint(x, pltpu.HBM)
            for x in (
                homolog_embedding,
                left_t,
                right_t,
                decoder,
                pair_output_bias.reshape(1, chan),
                pair_output_gradient.reshape(outer, inner * res, res, chan),
            )
        ]
    )
    first, second, align = pl.pallas_call(
        finish,
        out_shape=[
            jax.ShapeDtypeStruct((blk, rows), F32),
            jax.ShapeDtypeStruct((blk, rows), F32),
            jax.ShapeDtypeStruct((rows, res, width), BF16),
        ],
        in_specs=[vmem] * 3,
        out_specs=[vmem] * 3,
        scratch_shapes=[pltpu.VMEM((res, 2 * blk, width), BF16)],
        compiler_params=pltpu.CompilerParams(vmem_limit_bytes=16 * 1024 * 1024),
        name="finish",
    )(both, left_t, right_t)
    first = first.reshape(res, fac, rows).transpose(2, 0, 1)
    second = second.reshape(res, fac, rows).transpose(2, 0, 1)
    return first, second, align


def solution(mesh):
    placed = (P("group", "col", None), P(), P(), P(), P(), P("group", "col", None))
    return jax.shard_map(
        per_device,
        mesh=mesh,
        in_specs=placed,
        out_specs=(P("group", "col", None), P("group", "col", None), P("group", "col", None)),
        check_vma=False,
    )
```
